512 devices in a mesh: fsdp: 64 (over z_lo, x, core), tp: 8 (over z_hi, y).
Axes of the slice: x: 4, y: 4, z: 16 (z_hi: 2, z_lo: 8; z = z_hi * 8 + z_lo), core: 2. Of those that a mesh axis runs over, the one named last changes fastest.
Arguments:
- gradient: float32 [16384, 8192], P('fsdp', 'tp'), may hold values from -100 to 100
- sign_bits: int32 [8192, 128], P('tp'), may hold values 0 or 1
- block_column: int32 [64], P('tp'), may hold values from 0 to 3, as said below
Outputs:
- projected: float32 [512, 8192], P('fsdp', 'tp')
The draws below stay inside these ranges and needn't reach their ends.
Inputs may be any that keep to these rules, and one draw needn't show every extreme that they name: `block_column`: each of the 4 column blocks is chosen by at least two blocks of rows.
All inputs are finite; a program needn't handle non-finite values. No bound on the sum of `sign_bits` on one device may be relied on, other than what follows from the above.
Results may differ from the reference program's by a relative error of at most 0.000082.
Values sent between devices are 32-bit elements; how exact they have to be, the bound alone decides.
A program may use at most 64 MiB of HBM per device.

```python
import math
import jax
import jax.numpy as jnp
from jax import lax

M = 16384
N = 8192
R = 512
BLK = 128


def draw_gradient(key, part):
    keys = jax.random.split(jax.random.fold_in(key, 7), 2)
    row_scale = jnp.exp(jax.random.uniform(keys[1], (M, 1), jnp.float32) * math.log(10.0))
    values = row_scale * jnp.clip(jax.random.normal(keys[0], (M, N), jnp.float32), -6.0, 6.0)
    return values.astype(jnp.float32)


def draw_block_column(key, part):
    block_count = N // BLK
    column_blocks = R // BLK
    keys = jax.random.split(jax.random.fold_in(key, 11), 2)
    base = jax.random.randint(keys[0], (block_count,), 0, column_blocks, dtype=jnp.int32)
    shuffled = jax.random.permutation(keys[1], block_count)
    forced = jnp.arange(2 * column_blocks, dtype=jnp.int32) % column_blocks
    base = base.at[shuffled[:2 * column_blocks]].set(forced)
    return base.astype(jnp.int32)


def set_ends(drawn, rng, low, top_value):
    longest = drawn.shape.index(max(drawn.shape))
    spots = []
    for shift in (0, 1):
        where = [jax.random.randint(jax.random.fold_in(rng, axis), (), 0, length) for axis, length in enumerate(drawn.shape)]
        where[longest] = (where[longest] + shift) % drawn.shape[longest]
        spots.append(tuple(where))
    return drawn.at[spots[0]].set(low).at[spots[1]].set(top_value)


def setup_inputs(seed: int = 0) -> dict:
    splits = jax.random.split(jax.random.key(seed), 4)
    gradient = draw_gradient(jax.random.fold_in(splits[3], 71), 0)
    sign_bits = set_ends((jax.random.randint(splits[1], (N, BLK), 0, 2) < 1).astype(jnp.int32), jax.random.fold_in(splits[1], 1), 0, 1)
    block_column = draw_block_column(jax.random.fold_in(splits[3], 71), 0)
    return {"gradient": gradient, "sign_bits": sign_bits, "block_column": block_column}


def reference(gradient, sign_bits, block_column):
    block_count = N // BLK
    column_blocks = R // BLK
    sign_table = (2 * sign_bits - 1).astype(jnp.float32).reshape(block_count, BLK, BLK)
    row_blocks = gradient.reshape(M, block_count, BLK)
    mixture = jnp.einsum('rbk,bkj->rbj', row_blocks, sign_table, precision=lax.Precision.HIGHEST)
    chosen = (block_column[:, None] == jnp.arange(column_blocks, dtype=jnp.int32)[None, :]).astype(jnp.float32)
    sketch = jnp.einsum('rbj,bc->rcj', mixture, chosen, precision=lax.Precision.HIGHEST).reshape(M, R)
    gram_sum = jnp.dot(sketch.T.astype(jnp.float32), sketch.astype(jnp.float32), precision=lax.Precision.HIGHEST, preferred_element_type=jnp.float32)
    lower_factor = jnp.linalg.cholesky(gram_sum)
    basis_rows = jax.scipy.linalg.solve_triangular(lower_factor, sketch.T, lower=True).T
    return jnp.dot(basis_rows.T.astype(jnp.float32), gradient.astype(jnp.float32), precision=lax.Precision.HIGHEST, preferred_element_type=jnp.float32)
```

```python
import functools

import jax
import jax.numpy as jnp
from jax import lax
from jax.experimental import pallas as pl
from jax.experimental.pallas import tpu as pltpu
from jax.sharding import PartitionSpec as P

MESH = pl.DeviceIdType.MESH
HIGHEST = lax.Precision.HIGHEST
F32 = jnp.float32
BF16 = jnp.bfloat16

R = 512
BLK = 128
NZ, NX, NK, NY, NH = 8, 4, 2, 4, 2
NJ = NX * NK


def position():
    f = lax.axis_index("fsdp")
    t = lax.axis_index("tp")
    j = lax.rem(f, NJ)
    return f, t, lax.div(f, NJ), j, lax.div(j, NK), lax.rem(j, NK), lax.rem(t, NY), lax.div(t, NY)


def entry_barrier(peers):
    barrier = pltpu.get_barrier_semaphore()
    for peer in peers:
        pl.semaphore_signal(barrier, inc=1, device_id=peer, device_id_type=MESH)
    pl.semaphore_wait(barrier, len(peers))


class Sender:
    def __init__(self, send, recv):
        self.send, self.recv, self.copies = send, recv, []

    def put(self, src, dst, device):
        i = len(self.copies)
        copy = pltpu.make_async_remote_copy(
            src_ref=src,
            dst_ref=dst,
            send_sem=self.send.at[i],
            recv_sem=self.recv.at[i],
            device_id=device,
            device_id_type=MESH,
        )
        copy.start()
        self.copies.append(copy)
        return copy

    def drain(self):
        for copy in self.copies:
            copy.wait_send()


def arrive(copies):
    for copy in copies:
        copy.wait_recv()


def split(v):
    hi = v.astype(BF16)
    return hi, (v - hi.astype(F32)).astype(BF16)


def dot(a, b):
    return jnp.dot(a, b, preferred_element_type=F32)


def gather_kernel(
    bc_ref, g_ref, sb_ref, gram_ref, f_ref,
    om, ghi, glo, part, yrecv, q, zrecv, s, st, gp, gr, gz, gbuf, c, ck, d, dx, e, ez, send, recv,
):
    f, t, z, j, x, k, y, h = position()
    rows, cols = g_ref.shape

    def xk(dd):
        return lax.rem(j + dd, NJ)

    def zl(dd):
        return lax.rem(z + dd, NZ)

    def yl(dd):
        return lax.rem(y + dd, NY)

    def xl(dd):
        return lax.rem(x + dd, NX)

    peers = [(f, h * NY + yl(dd)) for dd in range(1, NY)]
    peers += [(f, (1 - h) * NY + y)]
    peers += [(z * NJ + xk(dd), t) for dd in range(1, NJ)]
    peers += [(zl(dd) * NJ + j, t) for dd in range(1, NZ)]
    entry_barrier(peers)
    net = Sender(send, recv)

    for b in range(cols // BLK):
        sign = (2 * sb_ref[b * BLK:(b + 1) * BLK, :] - 1).astype(F32)
        for cb in range(R // BLK):
            here = jnp.where(bc_ref[b] == cb, 1.0, 0.0).astype(F32)
            om[b * BLK:(b + 1) * BLK, cb * BLK:(cb + 1) * BLK] = (sign * here).astype(BF16)
    g = g_ref[...]
    hi, lo = split(g)
    ghi[...] = hi
    glo[...] = lo
    part[...] = (dot(ghi[...], om[...]) + dot(glo[...], om[...])).reshape(part.shape)

    stage = [net.put(part.at[yl(dd)], yrecv.at[dd - 1], (f, h * NY + yl(dd))) for dd in range(1, NY)]
    arrive(stage)
    q[...] = part[y] + yrecv[0] + yrecv[1] + yrecv[2]
    arrive([net.put(q, zrecv, (f, (1 - h) * NY + y))])
    s[y] = q[...] + zrecv[...]
    arrive([net.put(s.at[y], s.at[y], (f, h * NY + yl(dd))) for dd in range(1, NY)])

    whole = s[...].reshape(rows, R)
    st[...] = whole.T
    left = st[pl.ds(pl.multiple_of(y * 128, 128), 128), :]
    right = s[:, :, pl.ds(pl.multiple_of(h * 256, 256), 256)].reshape(rows, 256)
    gp[...] = jnp.dot(left, right, precision=HIGHEST, preferred_element_type=F32).reshape(gp.shape)
    gram_xk = [net.put(gp.at[xk(dd)], gr.at[dd - 1], (z * NJ + xk(dd), t)) for dd in range(1, NJ)]

    shi, slo = split(st[...])
    for n in range(cols // 256):
        gh, gl = ghi[:, n * 256:(n + 1) * 256], glo[:, n * 256:(n + 1) * 256]
        c[:, :, :, n * 256:(n + 1) * 256] = (dot(shi, gh) + (dot(shi, gl) + dot(slo, gh))).reshape(
            NX, NK, R // NJ, 256
        )
    c_k = net.put(c.at[:, 1 - k], ck, (z * NJ + x * NK + 1 - k, t))

    arrive(gram_xk)
    total = gp[j]
    for dd in range(1, NJ):
        total = total + gr[dd - 1]
    gz[z] = total
    gram_z = [net.put(gz.at[z], gz.at[z], (zl(dd) * NJ + j, t)) for dd in range(1, NZ)]

    arrive([c_k])
    d[...] = c[:, k] + ck[...]

    arrive(gram_z)
    total = gz[0]
    for i in range(1, NZ):
        total = total + gz[i]
    gbuf[h, y, x, k] = total
    arrive([net.put(gbuf.at[h, y, x, k], gbuf.at[h, y, x, k], (f, (1 - h) * NY + y))])
    arrive(
        [net.put(gbuf.at[:, y, x, k], gbuf.at[:, y, x, k], (f, h * NY + yl(dd))) for dd in range(1, NY)]
    )
    arrive(
        [
            net.put(gbuf.at[:, :, x, k], gbuf.at[:, :, x, k], (z * NJ + xl(dd) * NK + k, t))
            for dd in range(1, NX)
        ]
    )
    gram_k = net.put(gbuf.at[:, :, :, k], gbuf.at[:, :, :, k], (z * NJ + x * NK + 1 - k, t))

    c_x = [net.put(d.at[xl(dd)], dx.at[dd - 1], (z * NJ + xl(dd) * NK + k, t)) for dd in range(1, NX)]
    arrive([gram_k])
    gram_ref[...] = gbuf[...]
    arrive(c_x)
    slab = d[x] + dx[0] + dx[1] + dx[2]
    for n in range(NZ):
        e[n] = slab[:, n * BLK:(n + 1) * BLK]
    arrive([net.put(e.at[zl(dd)], ez.at[dd - 1], (zl(dd) * NJ + j, t)) for dd in range(1, NZ)])
    total = e[z]
    for dd in range(1, NZ):
        total = total + ez[dd - 1]
    f_ref[...] = total
    net.drain()


def scatter_kernel(y_ref, o_ref, yr, hz, ob, send, recv):
    f, t, z, j, x, k, y, h = position()

    def xk(dd):
        return lax.rem(j + dd, NJ)

    def zl(dd):
        return lax.rem(z + dd, NZ)

    entry_barrier(
        [(z * NJ + xk(dd), t) for dd in range(1, NJ)] + [(zl(dd) * NJ + j, t) for dd in range(1, NZ)]
    )
    net = Sender(send, recv)
    arrive([net.put(y_ref.at[:, xk(dd)], yr.at[dd - 1], (z * NJ + xk(dd), t)) for dd in range(1, NJ)])
    total = y_ref[:, j]
    for dd in range(1, NJ):
        total = total + yr[dd - 1]
    hz[...] = total
    ob[z] = hz[z]
    arrive([net.put(hz.at[zl(dd)], ob.at[z], (zl(dd) * NJ + j, t)) for dd in range(1, NZ)])
    for n in range(NZ):
        o_ref[:, n * BLK:(n + 1) * BLK] = ob[n]
    net.drain()


def shards(gradient, sign_bits, block_column):
    rows, cols = gradient.shape
    vmem = pl.BlockSpec(memory_space=pltpu.VMEM)
    n_sems = 64
    gram_shape = (NH, NY, NX, NK, 16, 256)
    gram, slab = pl.pallas_call(
        gather_kernel,
        out_shape=(
            jax.ShapeDtypeStruct(gram_shape, F32),
            jax.ShapeDtypeStruct((R // NJ, BLK), F32),
        ),
        in_specs=[pl.BlockSpec(memory_space=pltpu.SMEM), vmem, vmem],
        out_specs=(vmem, vmem),
        scratch_shapes=[
            pltpu.VMEM((cols, R), BF16),
            pltpu.VMEM((rows, cols), BF16),
            pltpu.VMEM((rows, cols), BF16),
            pltpu.VMEM((NY, rows // NY, R), F32),
            pltpu.VMEM((NY - 1, rows // NY, R), F32),
            pltpu.VMEM((rows // NY, R), F32),
            pltpu.VMEM((rows // NY, R), F32),
            pltpu.VMEM((NY, rows // NY, R), F32),
            pltpu.VMEM((R, rows), F32),
            pltpu.VMEM((NJ, 16, 256), F32),
            pltpu.VMEM((NJ - 1, 16, 256), F32),
            pltpu.VMEM((NZ, 16, 256), F32),
            pltpu.VMEM(gram_shape, F32),
            pltpu.VMEM((NX, NK, R // NJ, cols), F32),
            pltpu.VMEM((NX, R // NJ, cols), F32),
            pltpu.VMEM((NX, R // NJ, cols), F32),
            pltpu.VMEM((NX - 1, R // NJ, cols), F32),
            pltpu.VMEM((NZ, R // NJ, BLK), F32),
            pltpu.VMEM((NZ - 1, R // NJ, BLK), F32),
            pltpu.SemaphoreType.DMA((n_sems,)),
            pltpu.SemaphoreType.DMA((n_sems,)),
        ],
        compiler_params=pltpu.CompilerParams(
            collective_id=0, has_side_effects=True, vmem_limit_bytes=48 * 1024 * 1024
        ),
        name="gather",
    )(block_column, gradient, sign_bits)
    halves = gram.reshape(NH, R, 256)
    whole = jnp.concatenate([halves[0], halves[1]], axis=1)
    lower = jnp.linalg.cholesky(whole)
    j = lax.rem(lax.axis_index("fsdp"), NJ)
    rhs = lax.dynamic_update_slice(jnp.zeros((R, BLK), F32), slab, (j * (R // NJ), 0))
    solved = jax.scipy.linalg.solve_triangular(lower, rhs, lower=True)
    return pl.pallas_call(
        scatter_kernel,
        out_shape=jax.ShapeDtypeStruct((R // (NZ * NJ), cols), F32),
        in_specs=[vmem],
        out_specs=vmem,
        scratch_shapes=[
            pltpu.VMEM((NJ - 1, NZ, 8, BLK), F32),
            pltpu.VMEM((NZ, 8, BLK), F32),
            pltpu.VMEM((NZ, 8, BLK), F32),
            pltpu.SemaphoreType.DMA((NJ + NZ,)),
            pltpu.SemaphoreType.DMA((NJ + NZ,)),
        ],
        compiler_params=pltpu.CompilerParams(collective_id=1, has_side_effects=True),
        name="scatter",
    )(solved.reshape(NZ, NJ, 8, BLK))


def solution(mesh):
    return jax.shard_map(
        shards,
        mesh=mesh,
        in_specs=(P("fsdp", "tp"), P("tp", None), P("tp")),
        out_specs=P("fsdp", "tp"),
        check_vma=False,
    )
```

```python
import functools

import jax
import jax.numpy as jnp
from jax import lax
from jax.experimental import pallas as pl
from jax.experimental.pallas import tpu as pltpu
from jax.sharding import PartitionSpec as P

MESH = pl.DeviceIdType.MESH
HIGHEST = lax.Precision.HIGHEST
F32 = jnp.float32
BF16 = jnp.bfloat16

R = 512
BLK = 128
NZ, NX, NK, NY, NH = 8, 4, 2, 4, 2
NJ = NX * NK


def position():
    f = lax.axis_index("fsdp")
    t = lax.axis_index("tp")
    j = lax.rem(f, NJ)
    return f, t, lax.div(f, NJ), j, lax.div(j, NK), lax.rem(j, NK), lax.rem(t, NY), lax.div(t, NY)


def entry_barrier(peers):
    barrier = pltpu.get_barrier_semaphore()
    for peer in peers:
        pl.semaphore_signal(barrier, inc=1, device_id=peer, device_id_type=MESH)
    pl.semaphore_wait(barrier, len(peers))


class Sender:
    def __init__(self, send, recv):
        self.send, self.recv, self.copies = send, recv, []

    def put(self, src, dst, device):
        i = len(self.copies)
        copy = pltpu.make_async_remote_copy(
            src_ref=src,
            dst_ref=dst,
            send_sem=self.send.at[i],
            recv_sem=self.recv.at[i],
            device_id=device,
            device_id_type=MESH,
        )
        copy.start()
        self.copies.append(copy)
        return copy

    def drain(self):
        for copy in self.copies:
            copy.wait_send()


def arrive(copies):
    for copy in copies:
        copy.wait_recv()


def split(v):
    hi = v.astype(BF16)
    return hi, (v - hi.astype(F32)).astype(BF16)


def dot(a, b):
    return jnp.dot(a, b, preferred_element_type=F32)


def factor_block(a, ub, p):
    base = BLK * p
    tiles = (R + BLK - base) // BLK
    sub = lax.broadcasted_iota(jnp.int32, (8, BLK), 0)
    lane = lax.broadcasted_iota(jnp.int32, (8, BLK), 1)

    def spread(v):
        return jnp.broadcast_to(v, (8, BLK))

    def columns(tile):
        return slice(base + BLK * tile, base + BLK * (tile + 1))

    def panel(q, rows):
        here = pl.multiple_of(base + 8 * q, 8)
        following = pl.multiple_of(base + 8 * jnp.minimum(q + 1, BLK // 8 - 1), 8)
        rows = list(rows)
        keep = (lane >= 8 * (q + 1)) & (q > 0)
        coef = jnp.where(keep, -ub[:, columns(0)], 0.0).T
        for g in range(1, BLK // 8):
            ms = [spread(coef[8 * g:8 * g + 8, i:i + 1]) for i in range(8)]
            at = slice(base + 8 * g, base + 8 * g + 8)
            for tile in range(tiles):
                acc = a[at, columns(tile)]
                for i in range(8):
                    acc = acc + ms[i] * spread(ub[i:i + 1, columns(tile)])
                a[at, columns(tile)] = acc
        head = pltpu.roll(rows[0], BLK - 8 * q, 1)
        flip = head.T
        c = [spread(head[:, i:i + 1]) for i in range(8)]
        x = [spread(flip[8:16, i:i + 1]) for i in range(8)]
        ahead = [jnp.zeros((8, BLK), F32) for _ in range(tiles)]
        for i in range(8):
            rs = lax.rsqrt(spread(c[i][i:i + 1, :]))
            li, yi = c[i] * rs, x[i] * rs
            for kk in range(i + 1, 8):
                lk = spread(c[i][kk:kk + 1, :]) * rs
                c[kk] = c[kk] - li * lk
                x[kk] = x[kk] - yi * lk
            low = jnp.where(sub > i, li, 0.0)
            for tile in range(tiles):
                row = spread(rows[tile][i:i + 1, :]) * rs
                rows[tile] = jnp.where(sub == i, row, rows[tile] - low * row)
                ahead[tile] = ahead[tile] + yi * row
        out = []
        for tile in range(tiles):
            a[pl.ds(here, 8), columns(tile)] = rows[tile]
            ub[:, columns(tile)] = rows[tile]
            out.append(a[pl.ds(following, 8), columns(tile)] - ahead[tile])
        return tuple(out)

    first = tuple(a[base:base + 8, columns(tile)] for tile in range(tiles))
    lax.fori_loop(0, BLK // 8, panel, first)
    if base + BLK < R:
        below = slice(base + BLK, R)
        right = slice(base + BLK, R + BLK)
        done = slice(base, base + BLK)
        a[below, right] = a[below, right] - jnp.dot(
            a[done, below].T, a[done, right], precision=HIGHEST, preferred_element_type=F32
        )


def refresh_kernel(
    bc_ref, g_ref, sb_ref, o_ref,
    om, ghi, glo, part, yrecv, q, zrecv, s, st, gp, gr, gz, gbuf, c, ck, d, dx, e, ez,
    a, ub, yb, yr, hz, ob, send, recv,
):
    f, t, z, j, x, k, y, h = position()
    rows, cols = g_ref.shape

    def xk(dd):
        return lax.rem(j + dd, NJ)

    def zl(dd):
        return lax.rem(z + dd, NZ)

    def yl(dd):
        return lax.rem(y + dd, NY)

    def xl(dd):
        return lax.rem(x + dd, NX)

    peers = [(f, h * NY + yl(dd)) for dd in range(1, NY)]
    peers += [(f, (1 - h) * NY + y)]
    peers += [(z * NJ + xk(dd), t) for dd in range(1, NJ)]
    peers += [(zl(dd) * NJ + j, t) for dd in range(1, NZ)]
    entry_barrier(peers)
    net = Sender(send, recv)

    for b in range(cols // BLK):
        sign = (2 * sb_ref[b * BLK:(b + 1) * BLK, :] - 1).astype(F32)
        for cb in range(R // BLK):
            here = jnp.where(bc_ref[b] == cb, 1.0, 0.0).astype(F32)
            om[b * BLK:(b + 1) * BLK, cb * BLK:(cb + 1) * BLK] = (sign * here).astype(BF16)
    g = g_ref[...]
    hi, lo = split(g)
    ghi[...] = hi
    glo[...] = lo
    part[...] = (dot(ghi[...], om[...]) + dot(glo[...], om[...])).reshape(part.shape)

    stage = [net.put(part.at[yl(dd)], yrecv.at[dd - 1], (f, h * NY + yl(dd))) for dd in range(1, NY)]
    arrive(stage)
    q[...] = part[y] + yrecv[0] + yrecv[1] + yrecv[2]
    arrive([net.put(q, zrecv, (f, (1 - h) * NY + y))])
    s[y] = q[...] + zrecv[...]
    arrive([net.put(s.at[y], s.at[y], (f, h * NY + yl(dd))) for dd in range(1, NY)])

    whole = s[...].reshape(rows, R)
    st[...] = whole.T
    left = st[pl.ds(pl.multiple_of(y * 128, 128), 128), :]
    right = s[:, :, pl.ds(pl.multiple_of(h * 256, 256), 256)].reshape(rows, 256)
    gp[...] = jnp.dot(left, right, precision=HIGHEST, preferred_element_type=F32).reshape(gp.shape)
    gram_xk = [net.put(gp.at[xk(dd)], gr.at[dd - 1], (z * NJ + xk(dd), t)) for dd in range(1, NJ)]

    shi, slo = split(st[...])
    for n in range(cols // 256):
        gh, gl = ghi[:, n * 256:(n + 1) * 256], glo[:, n * 256:(n + 1) * 256]
        c[:, :, :, n * 256:(n + 1) * 256] = (dot(shi, gh) + (dot(shi, gl) + dot(slo, gh))).reshape(
            NX, NK, R // NJ, 256
        )
    c_k = net.put(c.at[:, 1 - k], ck, (z * NJ + x * NK + 1 - k, t))

    arrive(gram_xk)
    total = gp[j]
    for dd in range(1, NJ):
        total = total + gr[dd - 1]
    gz[z] = total
    gram_z = [net.put(gz.at[z], gz.at[z], (zl(dd) * NJ + j, t)) for dd in range(1, NZ)]

    arrive([c_k])
    d[...] = c[:, k] + ck[...]

    arrive(gram_z)
    total = gz[0]
    for i in range(1, NZ):
        total = total + gz[i]
    gbuf[h, y, x, k] = total
    arrive([net.put(gbuf.at[h, y, x, k], gbuf.at[h, y, x, k], (f, (1 - h) * NY + y))])
    arrive(
        [net.put(gbuf.at[:, y, x, k], gbuf.at[:, y, x, k], (f, h * NY + yl(dd))) for dd in range(1, NY)]
    )
    arrive(
        [
            net.put(gbuf.at[:, :, x, k], gbuf.at[:, :, x, k], (z * NJ + xl(dd) * NK + k, t))
            for dd in range(1, NX)
        ]
    )
    gram_k = net.put(gbuf.at[:, :, :, k], gbuf.at[:, :, :, k], (z * NJ + x * NK + 1 - k, t))

    c_x = [net.put(d.at[xl(dd)], dx.at[dd - 1], (z * NJ + xl(dd) * NK + k, t)) for dd in range(1, NX)]
    arrive([gram_k])

    for half in range(NH):
        a[:, half * 256:(half + 1) * 256] = gbuf[half].reshape(R, 256)
    chunk = R // NJ
    down = lax.broadcasted_iota(jnp.int32, (R, BLK), 0) - chunk * j
    across = lax.broadcasted_iota(jnp.int32, (R, BLK), 1)
    a[:, R:] = jnp.where((down == across) & (across < chunk), 1.0, 0.0)
    ub[...] = jnp.zeros_like(ub)
    factor_block(a, ub, 0)
    arrive(c_x)
    slab = d[x] + dx[0] + dx[1] + dx[2]
    for n in range(NZ):
        e[n] = slab[:, n * BLK:(n + 1) * BLK]
    c_z = [net.put(e.at[zl(dd)], ez.at[dd - 1], (zl(dd) * NJ + j, t)) for dd in range(1, NZ)]
    for p in range(1, R // BLK):
        factor_block(a, ub, p)
    arrive(c_z)
    total = e[z]
    for dd in range(1, NZ):
        total = total + ez[dd - 1]
    yb[...] = jnp.dot(
        a[:, R:R + chunk], total, precision=HIGHEST, preferred_element_type=F32
    ).reshape(yb.shape)

    arrive([net.put(yb.at[:, xk(dd)], yr.at[dd - 1], (z * NJ + xk(dd), t)) for dd in range(1, NJ)])
    total = yb[:, j]
    for dd in range(1, NJ):
        total = total + yr[dd - 1]
    hz[...] = total
    ob[z] = hz[z]
    arrive([net.put(hz.at[zl(dd)], ob.at[z], (zl(dd) * NJ + j, t)) for dd in range(1, NZ)])
    for n in range(NZ):
        o_ref[:, n * BLK:(n + 1) * BLK] = ob[n]
    net.drain()


def shards(gradient, sign_bits, block_column):
    rows, cols = gradient.shape
    vmem = pl.BlockSpec(memory_space=pltpu.VMEM)
    n_sems = 80
    gram_shape = (NH, NY, NX, NK, 16, 256)
    return pl.pallas_call(
        refresh_kernel,
        out_shape=jax.ShapeDtypeStruct((R // (NZ * NJ), cols), F32),
        in_specs=[pl.BlockSpec(memory_space=pltpu.SMEM), vmem, vmem],
        out_specs=vmem,
        scratch_shapes=[
            pltpu.VMEM((cols, R), BF16),
            pltpu.VMEM((rows, cols), BF16),
            pltpu.VMEM((rows, cols), BF16),
            pltpu.VMEM((NY, rows // NY, R), F32),
            pltpu.VMEM((NY - 1, rows // NY, R), F32),
            pltpu.VMEM((rows // NY, R), F32),
            pltpu.VMEM((rows // NY, R), F32),
            pltpu.VMEM((NY, rows // NY, R), F32),
            pltpu.VMEM((R, rows), F32),
            pltpu.VMEM((NJ, 16, 256), F32),
            pltpu.VMEM((NJ - 1, 16, 256), F32),
            pltpu.VMEM((NZ, 16, 256), F32),
            pltpu.VMEM(gram_shape, F32),
            pltpu.VMEM((NX, NK, R // NJ, cols), F32),
            pltpu.VMEM((NX, R // NJ, cols), F32),
            pltpu.VMEM((NX, R // NJ, cols), F32),
            pltpu.VMEM((NX - 1, R // NJ, cols), F32),
            pltpu.VMEM((NZ, R // NJ, BLK), F32),
            pltpu.VMEM((NZ - 1, R // NJ, BLK), F32),
            pltpu.VMEM((R, R + BLK), F32),
            pltpu.VMEM((8, R + BLK), F32),
            pltpu.VMEM((NZ, NJ, 8, BLK), F32),
            pltpu.VMEM((NJ - 1, NZ, 8, BLK), F32),
            pltpu.VMEM((NZ, 8, BLK), F32),
            pltpu.VMEM((NZ, 8, BLK), F32),
            pltpu.SemaphoreType.DMA((n_sems,)),
            pltpu.SemaphoreType.DMA((n_sems,)),
        ],
        compiler_params=pltpu.CompilerParams(
            collective_id=0, has_side_effects=True, vmem_limit_bytes=48 * 1024 * 1024
        ),
        name="refresh",
    )(block_column, gradient, sign_bits)


def solution(mesh):
    return jax.shard_map(
        shards,
        mesh=mesh,
        in_specs=(P("fsdp", "tp"), P("tp", None), P("tp")),
        out_specs=P("fsdp", "tp"),
        check_vma=False,
    )
```

```python
import functools

import jax
import jax.numpy as jnp
from jax import lax
from jax.experimental import pallas as pl
from jax.experimental.pallas import tpu as pltpu
from jax.sharding import PartitionSpec as P

MESH = pl.DeviceIdType.MESH
HIGHEST = lax.Precision.HIGHEST
F32 = jnp.float32
BF16 = jnp.bfloat16

R = 512
BLK = 128
SUB = 64
NZ, NX, NK, NY, NH = 8, 4, 2, 4, 2
NJ = NX * NK
NM = NY * NJ
NT = NH * NZ


def position():
    f = lax.axis_index("fsdp")
    t = lax.axis_index("tp")
    j = lax.rem(f, NJ)
    return f, t, lax.div(f, NJ), j, lax.div(j, NK), lax.rem(j, NK), lax.rem(t, NY), lax.div(t, NY)


class Sender:
    def __init__(self, send, recv):
        self.send, self.recv, self.copies = send, recv, []

    def put(self, src, dst, device):
        i = len(self.copies)
        copy = pltpu.make_async_remote_copy(
            src_ref=src,
            dst_ref=dst,
            send_sem=self.send.at[i],
            recv_sem=self.recv.at[i],
            device_id=device,
            device_id_type=MESH,
        )
        copy.start()
        self.copies.append(copy)
        return copy

    def drain(self):
        for copy in self.copies:
            copy.wait_send()


def arrive(copies):
    for copy in copies:
        copy.wait_recv()


def split(v):
    hi = v.astype(BF16)
    return hi, (v - hi.astype(F32)).astype(BF16)


def dot(a, b):
    return jnp.dot(a, b, preferred_element_type=F32)


def strip(a, base, at):
    sub = lax.broadcasted_iota(jnp.int32, (8, BLK), 0)
    groups, tiles, lead = SUB // 8, (R + BLK - base) // BLK, at - base

    def spread(v):
        return jnp.broadcast_to(v, (8, BLK))

    def place(g, tile):
        return slice(at + 8 * g, at + 8 * g + 8), slice(base + BLK * tile, base + BLK * (tile + 1))

    rows = [[a[place(g, tile)] for tile in range(tiles)] for g in range(groups)]
    for g in range(groups):
        later = range(groups - g)
        lane = lead + 8 * g
        col = [[spread(rows[g + w][0][:, lane + i:lane + i + 1]) for i in range(8)] for w in later]
        for i in range(8):
            rs = lax.rsqrt(spread(col[0][i][i:i + 1, :]))
            l = [col[w][i] * rs for w in later]
            for n in range(i + 1, 8):
                ln = spread(col[0][i][n:n + 1, :]) * rs
                for w in later:
                    col[w][n] = col[w][n] - l[w] * ln
            low = jnp.where(sub > i, l[0], 0.0)
            for tile in range(tiles):
                row = spread(rows[g][tile][i:i + 1, :]) * rs
                rows[g][tile] = jnp.where(sub == i, row, rows[g][tile] - low * row)
                for w in later[1:]:
                    rows[g + w][tile] = rows[g + w][tile] - l[w] * row
    for g in range(groups):
        for tile in range(tiles):
            a[place(g, tile)] = rows[g][tile]


def take_off(a, done, rest, right):
    a[rest, right] = a[rest, right] - jnp.dot(
        a[done, rest].T, a[done, right], precision=HIGHEST, preferred_element_type=F32
    )


def factor(a):
    end = R + BLK
    for base in range(0, R, BLK):
        for at in range(base, base + BLK, SUB):
            strip(a, base, at)
            if at + SUB < base + BLK:
                take_off(a, slice(at, at + SUB), slice(at + SUB, base + BLK), slice(base, end))
        if base + BLK < R:
            take_off(a, slice(base, base + BLK), slice(base + BLK, R), slice(base + BLK, end))


def refresh_kernel(
    bc_ref, g_hbm, sb_hbm, o_ref,
    g_ref, sb_ref, om, ghi, glo, part, yrecv, q, zrecv, s, st, gp, gr, gz, gbuf, c, ck, d, dx, e, ez,
    a, yb, yr, hz, ob, send, recv, local,
):
    f, t, z, j, x, k, y, h = position()
    rows, cols = g_ref.shape
    m, zz = y * NJ + j, h * NZ + z

    def at_z(dd):
        w = lax.rem(zz + dd, NT)
        return lax.rem(w, NZ) * NJ + j, lax.div(w, NZ) * NY + y

    def zl(dd):
        return lax.rem(z + dd, NZ)

    def at_zl(dd):
        return zl(dd) * NJ + j, t

    def ml(dd):
        return lax.rem(m + dd, NM)

    def at_m(dd):
        w = ml(dd)
        return z * NJ + lax.rem(w, NJ), h * NY + lax.div(w, NJ)

    def jl(dd):
        return lax.rem(j + dd, NJ)

    def at_j(dd):
        return z * NJ + jl(dd), t

    def yl(dd):
        return lax.rem(y + dd, NY)

    def at_y(dd):
        return f, h * NY + yl(dd)

    def xl(dd):
        return lax.rem(x + dd, NX)

    def at_yx(dy, dx):
        return z * NJ + xl(dx) * NK + k, h * NY + yl(dy)

    partner = (z * NJ + x * NK + 1 - k, t)
    loads = [
        pltpu.make_async_copy(g_hbm, g_ref, local.at[0]),
        pltpu.make_async_copy(sb_hbm, sb_ref, local.at[1]),
    ]
    for load in loads:
        load.start()
    peers = [at_m(dd) for dd in range(1, NM)] + [at_z(dd) for dd in range(1, NT)]
    barrier = pltpu.get_barrier_semaphore()
    for peer in peers:
        pl.semaphore_signal(barrier, inc=1, device_id=peer, device_id_type=MESH)

    for load in loads:
        load.wait()
    for b in range(cols // BLK):
        sign = (2 * sb_ref[b * BLK:(b + 1) * BLK, :] - 1).astype(F32)
        for cb in range(R // BLK):
            here = jnp.where(bc_ref[b] == cb, 1.0, 0.0).astype(F32)
            om[b * BLK:(b + 1) * BLK, cb * BLK:(cb + 1) * BLK] = (sign * here).astype(BF16)
    hi, lo = split(g_ref[...])
    ghi[...] = hi
    glo[...] = lo
    part[...] = (dot(ghi[...], om[...]) + dot(glo[...], om[...])).reshape(part.shape)
    pl.semaphore_wait(barrier, len(peers))
    net = Sender(send, recv)

    arrive([net.put(part.at[yl(dd)], yrecv.at[dd - 1], at_y(dd)) for dd in range(1, NY)])
    q[...] = part[y] + yrecv[0] + yrecv[1] + yrecv[2]
    arrive([net.put(q, zrecv, at_z(NZ))])
    mine = q[...] + zrecv[...]
    s[y] = mine

    right = s[y, :, pl.ds(pl.multiple_of(h * 256, 256), 256)]
    gp[...] = jnp.dot(mine.T, right, precision=HIGHEST, preferred_element_type=F32).reshape(gp.shape)
    gram_m = [net.put(gp.at[ml(dd)], gr.at[dd - 1], at_m(dd)) for dd in range(1, NM)]
    slab = [net.put(s.at[y], s.at[y], at_y(dd)) for dd in range(1, NY)]
    arrive(gram_m)
    total = gp[m]
    for dd in range(1, NM):
        total = total + gr[dd - 1]
    gz[h, z] = total
    gram_z = [net.put(gz.at[h, z], gz.at[h, z], at_z(dd)) for dd in range(1, NT)]

    arrive(slab)
    st[...] = s[...].reshape(rows, R).T
    shi, slo = split(st[...])
    for n in range(cols // 256):
        gh, gl = ghi[:, n * 256:(n + 1) * 256], glo[:, n * 256:(n + 1) * 256]
        c[:, :, :, n * 256:(n + 1) * 256] = (dot(shi, gh) + (dot(shi, gl) + dot(slo, gh))).reshape(
            NX, NK, R // NJ, 256
        )
    arrive([net.put(c.at[:, 1 - k], ck, partner)])
    d[...] = c[:, k] + ck[...]
    c_x = [net.put(d.at[xl(dd)], dx.at[dd - 1], at_yx(0, dd)) for dd in range(1, NX)]

    arrive(gram_z)
    for half in range(NH):
        total = gz[half, 0]
        for i in range(1, NZ):
            total = total + gz[half, i]
        gbuf[half, y, x, k] = total
    near = [(dy, dd) for dy in range(NY) for dd in range(NX) if dy or dd]
    gram_yx = [net.put(gbuf.at[:, y, x, k], gbuf.at[:, y, x, k], at_yx(dy, dd)) for dy, dd in near]
    gram_k = [net.put(gbuf.at[:, y, x, k], gbuf.at[:, y, x, k], partner)]
    for (dy, dd), copy in zip(near, gram_yx):
        copy.wait_recv()
        ys, xs = lax.rem(y + NY - dy, NY), lax.rem(x + NX - dd, NX)
        gram_k.append(net.put(gbuf.at[:, ys, xs, k], gbuf.at[:, ys, xs, k], partner))
    arrive(c_x)
    total = d[x] + dx[0] + dx[1] + dx[2]
    for n in range(NZ):
        e[n] = total[:, n * BLK:(n + 1) * BLK]
    c_z = [net.put(e.at[zl(dd)], ez.at[dd - 1], at_zl(dd)) for dd in range(1, NZ)]
    arrive(gram_k)

    for half in range(NH):
        a[:, half * 256:(half + 1) * 256] = gbuf[half].reshape(R, 256)
    chunk = R // NJ
    down = lax.broadcasted_iota(jnp.int32, (R, BLK), 0) - chunk * j
    across = lax.broadcasted_iota(jnp.int32, (R, BLK), 1)
    a[:, R:] = jnp.where((down == across) & (across < chunk), 1.0, 0.0)
    factor(a)
    arrive(c_z)
    total = e[z]
    for dd in range(1, NZ):
        total = total + ez[dd - 1]
    yb[...] = jnp.dot(
        a[:, R:R + chunk], total, precision=HIGHEST, preferred_element_type=F32
    ).reshape(yb.shape)

    arrive([net.put(yb.at[:, jl(dd)], yr.at[dd - 1], at_j(dd)) for dd in range(1, NJ)])
    total = yb[:, j]
    for dd in range(1, NJ):
        total = total + yr[dd - 1]
    hz[...] = total
    ob[z] = hz[z]
    arrive([net.put(hz.at[zl(dd)], ob.at[z], at_zl(dd)) for dd in range(1, NZ)])
    for n in range(NZ):
        o_ref[:, n * BLK:(n + 1) * BLK] = ob[n]
    net.drain()


def shards(gradient, sign_bits, block_column):
    rows, cols = gradient.shape
    vmem = pl.BlockSpec(memory_space=pltpu.VMEM)
    hbm = pl.BlockSpec(memory_space=pltpu.HBM)
    n_sems = 128
    gram_shape = (NH, NY, NX, NK, 16, 256)
    return pl.pallas_call(
        refresh_kernel,
        out_shape=jax.ShapeDtypeStruct((R // (NZ * NJ), cols), F32),
        in_specs=[pl.BlockSpec(memory_space=pltpu.SMEM), hbm, hbm],
        out_specs=vmem,
        scratch_shapes=[
            pltpu.VMEM((rows, cols), F32),
            pltpu.VMEM((cols, BLK), jnp.int32),
            pltpu.VMEM((cols, R), BF16),
            pltpu.VMEM((rows, cols), BF16),
            pltpu.VMEM((rows, cols), BF16),
            pltpu.VMEM((NY, rows // NY, R), F32),
            pltpu.VMEM((NY - 1, rows // NY, R), F32),
            pltpu.VMEM((rows // NY, R), F32),
            pltpu.VMEM((rows // NY, R), F32),
            pltpu.VMEM((NY, rows // NY, R), F32),
            pltpu.VMEM((R, rows), F32),
            pltpu.VMEM((NM, 16, 256), F32),
            pltpu.VMEM((NM - 1, 16, 256), F32),
            pltpu.VMEM((NH, NZ, 16, 256), F32),
            pltpu.VMEM(gram_shape, F32),
            pltpu.VMEM((NX, NK, R // NJ, cols), F32),
            pltpu.VMEM((NX, R // NJ, cols), F32),
            pltpu.VMEM((NX, R // NJ, cols), F32),
            pltpu.VMEM((NX - 1, R // NJ, cols), F32),
            pltpu.VMEM((NZ, R // NJ, BLK), F32),
            pltpu.VMEM((NZ - 1, R // NJ, BLK), F32),
            pltpu.VMEM((R, R + BLK), F32),
            pltpu.VMEM((NZ, NJ, 8, BLK), F32),
            pltpu.VMEM((NJ - 1, NZ, 8, BLK), F32),
            pltpu.VMEM((NZ, 8, BLK), F32),
            pltpu.VMEM((NZ, 8, BLK), F32),
            pltpu.SemaphoreType.DMA((n_sems,)),
            pltpu.SemaphoreType.DMA((n_sems,)),
            pltpu.SemaphoreType.DMA((2,)),
        ],
        compiler_params=pltpu.CompilerParams(
            collective_id=0, has_side_effects=True
        ),
        name="refresh",
    )(block_column, gradient, sign_bits)


def solution(mesh):
    return jax.shard_map(
        shards,
        mesh=mesh,
        in_specs=(P("fsdp", "tp"), P("tp", None), P("tp")),
        out_specs=P("fsdp", "tp"),
        check_vma=False,
    )
```

```python
import functools

import jax
import jax.numpy as jnp
from jax import lax
from jax.experimental import pallas as pl
from jax.experimental.pallas import tpu as pltpu
from jax.sharding import PartitionSpec as P

MESH = pl.DeviceIdType.MESH
HIGHEST = lax.Precision.HIGHEST
F32 = jnp.float32
BF16 = jnp.bfloat16

R = 512
BLK = 128
SUB = 64
NZ, NX, NK, NY, NH = 8, 4, 2, 4, 2
NJ = NX * NK
NM = NY * NJ
NB = R // BLK
NT = NH * NZ


def position():
    f = lax.axis_index("fsdp")
    t = lax.axis_index("tp")
    j = lax.rem(f, NJ)
    return f, t, lax.div(f, NJ), j, lax.div(j, NK), lax.rem(j, NK), lax.rem(t, NY), lax.div(t, NY)


class Sender:
    def __init__(self, send, recv):
        self.send, self.recv, self.copies = send, recv, []

    def put(self, src, dst, device):
        i = len(self.copies)
        copy = pltpu.make_async_remote_copy(
            src_ref=src,
            dst_ref=dst,
            send_sem=self.send.at[i],
            recv_sem=self.recv.at[i],
            device_id=device,
            device_id_type=MESH,
        )
        copy.start()
        self.copies.append(copy)
        return copy

    def drain(self):
        for copy in self.copies:
            copy.wait_send()


def arrive(copies):
    for copy in copies:
        copy.wait_recv()


def split(v):
    hi = v.astype(BF16)
    return hi, (v - hi.astype(F32)).astype(BF16)


def dot(a, b):
    return jnp.dot(a, b, preferred_element_type=F32)


def strip(a, base, at):
    sub = lax.broadcasted_iota(jnp.int32, (8, BLK), 0)
    groups, tiles, lead = SUB // 8, (R + BLK - base) // BLK, at - base

    def spread(v):
        return jnp.broadcast_to(v, (8, BLK))

    def place(g, tile):
        return slice(at + 8 * g, at + 8 * g + 8), slice(base + BLK * tile, base + BLK * (tile + 1))

    rows = [[a[place(g, tile)] for tile in range(tiles)] for g in range(groups)]
    for g in range(groups):
        later = range(groups - g)
        lane = lead + 8 * g
        col = [[spread(rows[g + w][0][:, lane + i:lane + i + 1]) for i in range(8)] for w in later]
        for i in range(8):
            rs = lax.rsqrt(spread(col[0][i][i:i + 1, :]))
            l = [col[w][i] * rs for w in later]
            for n in range(i + 1, 8):
                ln = spread(col[0][i][n:n + 1, :]) * rs
                for w in later:
                    col[w][n] = col[w][n] - l[w] * ln
            low = jnp.where(sub > i, l[0], 0.0)
            for tile in range(tiles):
                row = spread(rows[g][tile][i:i + 1, :]) * rs
                rows[g][tile] = jnp.where(sub == i, row, rows[g][tile] - low * row)
                for w in later[1:]:
                    rows[g + w][tile] = rows[g + w][tile] - l[w] * row
    for g in range(groups):
        for tile in range(tiles):
            a[place(g, tile)] = rows[g][tile]


def owned(w):
    if w < 16:
        return [(0, w, 0), (0, w, 1), (0, w, 2), (0, w, 3), (3, 15 - w, 3)]
    return [(1, w - 16, 1), (1, w - 16, 2), (1, w - 16, 3), (2, 31 - w, 2), (2, 31 - w, 3)]


def take_off(a, done, rest, right):
    a[rest, right] = a[rest, right] - jnp.dot(
        a[done, rest].T, a[done, right], precision=HIGHEST, preferred_element_type=F32
    )


def factor(a):
    end = R + BLK
    for base in range(0, R, BLK):
        for at in range(base, base + BLK, SUB):
            strip(a, base, at)
            if at + SUB < base + BLK:
                take_off(a, slice(at, at + SUB), slice(at + SUB, base + BLK), slice(base, end))
        if base + BLK < R:
            take_off(a, slice(base, base + BLK), slice(base + BLK, R), slice(base + BLK, end))


def refresh_kernel(
    bc_ref, g_hbm, sb_hbm, o_ref,
    g_ref, sb_ref, om, ghi, glo, part, yrecv, q, zrecv, s, st, gp, gr, gz, gbuf, c, ck, d, dx, e, ez,
    a, yb, yr, hz, ob, send, recv, local,
):
    f, t, z, j, x, k, y, h = position()
    rows, cols = g_ref.shape
    m, zz = y * NJ + j, h * NZ + z

    def at_z(dd):
        w = lax.rem(zz + dd, NT)
        return lax.rem(w, NZ) * NJ + j, lax.div(w, NZ) * NY + y

    def zl(dd):
        return lax.rem(z + dd, NZ)

    def at_zl(dd):
        return zl(dd) * NJ + j, t

    def ml(dd):
        return lax.rem(m + dd, NM)

    def at_m(dd):
        w = ml(dd)
        return z * NJ + lax.rem(w, NJ), h * NY + lax.div(w, NJ)

    def jl(dd):
        return lax.rem(j + dd, NJ)

    def at_j(dd):
        return z * NJ + jl(dd), t

    def yl(dd):
        return lax.rem(y + dd, NY)

    def at_y(dd):
        return f, h * NY + yl(dd)

    def xl(dd):
        return lax.rem(x + dd, NX)

    def at_yx(dy, dx):
        return z * NJ + xl(dx) * NK + k, h * NY + yl(dy)

    partner = (z * NJ + x * NK + 1 - k, t)
    loads = [
        pltpu.make_async_copy(g_hbm, g_ref, local.at[0]),
        pltpu.make_async_copy(sb_hbm, sb_ref, local.at[1]),
    ]
    for load in loads:
        load.start()
    peers = [at_m(dd) for dd in range(1, NM)] + [at_z(dd) for dd in range(1, NT)]
    barrier = pltpu.get_barrier_semaphore()
    for peer in peers:
        pl.semaphore_signal(barrier, inc=1, device_id=peer, device_id_type=MESH)

    for load in loads:
        load.wait()
    for b in range(cols // BLK):
        sign = (2 * sb_ref[b * BLK:(b + 1) * BLK, :] - 1).astype(F32)
        for cb in range(R // BLK):
            here = jnp.where(bc_ref[b] == cb, 1.0, 0.0).astype(F32)
            om[b * BLK:(b + 1) * BLK, cb * BLK:(cb + 1) * BLK] = (sign * here).astype(BF16)
    hi, lo = split(g_ref[...])
    ghi[...] = hi
    glo[...] = lo
    for b in range(NB):
        pick = slice(b * BLK, (b + 1) * BLK)
        part[b] = (dot(ghi[...], om[:, pick]) + dot(glo[...], om[:, pick])).reshape(NY, rows // NY, BLK)
    pl.semaphore_wait(barrier, len(peers))
    net = Sender(send, recv)

    order = (2, 1, 3)
    over_y = [
        [net.put(part.at[b, yl(dd)], yrecv.at[b, dd - 1], at_y(dd)) for dd in order] for b in range(NB)
    ]
    over_z = []
    for b in range(NB):
        arrive(over_y[b])
        q[b] = part[b, y] + yrecv[b, 0] + yrecv[b, 1] + yrecv[b, 2]
        over_z.append(net.put(q.at[b], zrecv.at[b], at_z(NZ)))
    slab = []
    mine = []
    for b in range(NB):
        arrive([over_z[b]])
        mine.append(q[b] + zrecv[b])
        s[b, y] = mine[b]
        if b < 2:
            slab += [net.put(s.at[b, y], s.at[b, y], at_y(dd)) for dd in order]

    upper = [
        jnp.dot(
            mine[b].T,
            jnp.concatenate(mine[b:], axis=1),
            precision=HIGHEST,
            preferred_element_type=F32,
        )
        for b in range(NB)
    ]
    first_half = (jnp.zeros((8, BLK), jnp.int32) + h) == 0
    for w in range(NM):
        tiles = [upper[rb][8 * r:8 * r + 8, (cb - rb) * BLK:(cb - rb + 1) * BLK] for rb, r, cb in owned(w)]
        gp[w, 0] = jnp.where(first_half, tiles[0], tiles[3])
        gp[w, 1] = jnp.where(first_half, tiles[1], tiles[4])
        gp[w, 2] = jnp.where(first_half, tiles[2], 0.0)
    gram_m = [net.put(gp.at[ml(dd)], gr.at[dd - 1], at_m(dd)) for dd in range(1, NM)]
    for b in range(2, NB):
        slab += [net.put(s.at[b, y], s.at[b, y], at_y(dd)) for dd in order]
    arrive(gram_m)
    total = gp[m]
    for dd in range(1, NM):
        total = total + gr[dd - 1]
    gz[h, z] = total
    gram_z = [net.put(gz.at[h, z], gz.at[h, z], at_z(dd)) for dd in range(1, NT)]

    arrive(slab)
    for b in range(NB):
        st[b * BLK:(b + 1) * BLK, :] = s[b].reshape(rows, BLK).T
    shi, slo = split(st[...])
    for n in range(cols // 256):
        gh, gl = ghi[:, n * 256:(n + 1) * 256], glo[:, n * 256:(n + 1) * 256]
        c[:, :, :, n * 256:(n + 1) * 256] = (dot(shi, gh) + (dot(shi, gl) + dot(slo, gh))).reshape(
            NX, NK, R // NJ, 256
        )
    arrive([net.put(c.at[:, 1 - k], ck, partner)])
    d[...] = c[:, k] + ck[...]
    c_x = [net.put(d.at[xl(dd)], dx.at[dd - 1], at_yx(0, dd)) for dd in range(1, NX)]

    arrive(gram_z)
    for half in range(NH):
        total = gz[half, 0]
        for i in range(1, NZ):
            total = total + gz[half, i]
        gbuf[half, y, x, k] = total
    near = [(dy, dd) for dy in range(NY) for dd in range(NX) if dy or dd]
    gram_yx = [net.put(gbuf.at[:, y, x, k], gbuf.at[:, y, x, k], at_yx(dy, dd)) for dy, dd in near]
    gram_k = [net.put(gbuf.at[:, y, x, k], gbuf.at[:, y, x, k], partner)]
    for (dy, dd), copy in zip(near, gram_yx):
        copy.wait_recv()
        ys, xs = lax.rem(y + NY - dy, NY), lax.rem(x + NX - dd, NX)
        gram_k.append(net.put(gbuf.at[:, ys, xs, k], gbuf.at[:, ys, xs, k], partner))
    arrive(c_x)
    total = d[x] + dx[0] + dx[1] + dx[2]
    for n in range(NZ):
        e[n] = total[:, n * BLK:(n + 1) * BLK]
    c_z = [net.put(e.at[zl(dd)], ez.at[dd - 1], at_zl(dd)) for dd in range(1, NZ)]
    arrive(gram_k)

    for b in range(1, NB):
        a[b * BLK:(b + 1) * BLK, 0:b * BLK] = jnp.zeros((BLK, b * BLK), F32)
    for w in range(NM):
        from_m = w // NJ, w // NK % NX, w % NK
        for n, (rb, r, cb) in enumerate(owned(w)):
            at = rb * BLK + 8 * r
            a[at:at + 8, cb * BLK:(cb + 1) * BLK] = gbuf[(n // 3, *from_m, n % 3)]
    chunk = R // NJ
    down = lax.broadcasted_iota(jnp.int32, (R, BLK), 0) - chunk * j
    across = lax.broadcasted_iota(jnp.int32, (R, BLK), 1)
    a[:, R:] = jnp.where((down == across) & (across < chunk), 1.0, 0.0)
    factor(a)
    arrive(c_z)
    total = e[z]
    for dd in range(1, NZ):
        total = total + ez[dd - 1]
    yb[...] = jnp.dot(
        a[:, R:R + chunk], total, precision=HIGHEST, preferred_element_type=F32
    ).reshape(yb.shape)

    arrive([net.put(yb.at[:, jl(dd)], yr.at[dd - 1], at_j(dd)) for dd in range(1, NJ)])
    total = yb[:, j]
    for dd in range(1, NJ):
        total = total + yr[dd - 1]
    hz[...] = total
    ob[z] = hz[z]
    arrive([net.put(hz.at[zl(dd)], ob.at[z], at_zl(dd)) for dd in range(1, NZ)])
    for n in range(NZ):
        o_ref[:, n * BLK:(n + 1) * BLK] = ob[n]
    net.drain()


def shards(gradient, sign_bits, block_column):
    rows, cols = gradient.shape
    vmem = pl.BlockSpec(memory_space=pltpu.VMEM)
    hbm = pl.BlockSpec(memory_space=pltpu.HBM)
    n_sems = 144
    gram_shape = (NH, NY, NX, NK, 3, 8, BLK)
    return pl.pallas_call(
        refresh_kernel,
        out_shape=jax.ShapeDtypeStruct((R // (NZ * NJ), cols), F32),
        in_specs=[pl.BlockSpec(memory_space=pltpu.SMEM), hbm, hbm],
        out_specs=vmem,
        scratch_shapes=[
            pltpu.VMEM((rows, cols), F32),
            pltpu.VMEM((cols, BLK), jnp.int32),
            pltpu.VMEM((cols, R), BF16),
            pltpu.VMEM((rows, cols), BF16),
            pltpu.VMEM((rows, cols), BF16),
            pltpu.VMEM((NB, NY, rows // NY, BLK), F32),
            pltpu.VMEM((NB, NY - 1, rows // NY, BLK), F32),
            pltpu.VMEM((NB, rows // NY, BLK), F32),
            pltpu.VMEM((NB, rows // NY, BLK), F32),
            pltpu.VMEM((NB, NY, rows // NY, BLK), F32),
            pltpu.VMEM((R, rows), F32),
            pltpu.VMEM((NM, 3, 8, BLK), F32),
            pltpu.VMEM((NM - 1, 3, 8, BLK), F32),
            pltpu.VMEM((NH, NZ, 3, 8, BLK), F32),
            pltpu.VMEM(gram_shape, F32),
            pltpu.VMEM((NX, NK, R // NJ, cols), F32),
            pltpu.VMEM((NX, R // NJ, cols), F32),
            pltpu.VMEM((NX, R // NJ, cols), F32),
            pltpu.VMEM((NX - 1, R // NJ, cols), F32),
            pltpu.VMEM((NZ, R // NJ, BLK), F32),
            pltpu.VMEM((NZ - 1, R // NJ, BLK), F32),
            pltpu.VMEM((R, R + BLK), F32),
            pltpu.VMEM((NZ, NJ, 8, BLK), F32),
            pltpu.VMEM((NJ - 1, NZ, 8, BLK), F32),
            pltpu.VMEM((NZ, 8, BLK), F32),
            pltpu.VMEM((NZ, 8, BLK), F32),
            pltpu.SemaphoreType.DMA((n_sems,)),
            pltpu.SemaphoreType.DMA((n_sems,)),
            pltpu.SemaphoreType.DMA((2,)),
        ],
        compiler_params=pltpu.CompilerParams(
            collective_id=0, has_side_effects=True
        ),
        name="refresh",
    )(block_column, gradient, sign_bits)


def solution(mesh):
    return jax.shard_map(
        shards,
        mesh=mesh,
        in_specs=(P("fsdp", "tp"), P("tp", None), P("tp")),
        out_specs=P("fsdp", "tp"),
        check_vma=False,
    )
```

```python
import functools

import jax
import jax.numpy as jnp
from jax import lax
from jax.experimental import pallas as pl
from jax.experimental.pallas import tpu as pltpu
from jax.sharding import PartitionSpec as P

MESH = pl.DeviceIdType.MESH
HIGHEST = lax.Precision.HIGHEST
F32 = jnp.float32
BF16 = jnp.bfloat16

R = 512
BLK = 128
SUB = 64
NZ, NX, NK, NY, NH = 8, 4, 2, 4, 2
NJ = NX * NK
NM = NY * NJ
NB = R // BLK
NT = NH * NZ


def position():
    f = lax.axis_index("fsdp")
    t = lax.axis_index("tp")
    j = lax.rem(f, NJ)
    return f, t, lax.div(f, NJ), j, lax.div(j, NK), lax.rem(j, NK), lax.rem(t, NY), lax.div(t, NY)


class Sender:
    def __init__(self, send, recv):
        self.send, self.recv, self.copies = send, recv, []

    def put(self, src, dst, device):
        i = len(self.copies)
        copy = pltpu.make_async_remote_copy(
            src_ref=src,
            dst_ref=dst,
            send_sem=self.send.at[i],
            recv_sem=self.recv.at[i],
            device_id=device,
            device_id_type=MESH,
        )
        copy.start()
        self.copies.append(copy)
        return copy

    def drain(self):
        for copy in self.copies:
            copy.wait_send()


def arrive(copies):
    for copy in copies:
        copy.wait_recv()


def split(v):
    hi = v.astype(BF16)
    return hi, (v - hi.astype(F32)).astype(BF16)


def dot(a, b):
    return jnp.dot(a, b, preferred_element_type=F32)


def strip(a, base, at):
    sub = lax.broadcasted_iota(jnp.int32, (8, BLK), 0)
    groups, tiles, lead = SUB // 8, (R + BLK - base) // BLK, at - base

    def spread(v):
        return jnp.broadcast_to(v, (8, BLK))

    def place(g, tile):
        return slice(at + 8 * g, at + 8 * g + 8), slice(base + BLK * tile, base + BLK * (tile + 1))

    rows = [[a[place(g, tile)] for tile in range(tiles)] for g in range(groups)]
    for g in range(groups):
        later = range(groups - g)
        lane = lead + 8 * g
        col = [[spread(rows[g + w][0][:, lane + i:lane + i + 1]) for i in range(8)] for w in later]
        for i in range(8):
            rs = lax.rsqrt(spread(col[0][i][i:i + 1, :]))
            l = [col[w][i] * rs for w in later]
            for n in range(i + 1, 8):
                ln = spread(col[0][i][n:n + 1, :]) * rs
                for w in later:
                    col[w][n] = col[w][n] - l[w] * ln
            low = jnp.where(sub > i, l[0], 0.0)
            for tile in range(tiles):
                row = spread(rows[g][tile][i:i + 1, :]) * rs
                rows[g][tile] = jnp.where(sub == i, row, rows[g][tile] - low * row)
                for w in later[1:]:
                    rows[g + w][tile] = rows[g + w][tile] - l[w] * row
    for g in range(groups):
        for tile in range(tiles):
            a[place(g, tile)] = rows[g][tile]


def owned(w):
    if w < 16:
        return [(0, w, 0), (0, w, 1), (0, w, 2), (0, w, 3), (3, 15 - w, 3)]
    return [(1, w - 16, 1), (1, w - 16, 2), (1, w - 16, 3), (2, 31 - w, 2), (2, 31 - w, 3)]


def take_off(a, done, rest, right):
    a[rest, right] = a[rest, right] - jnp.dot(
        a[done, rest].T, a[done, right], precision=HIGHEST, preferred_element_type=F32
    )


def factor(a, base):
    end = R + BLK
    for at in range(base, base + BLK, SUB):
        strip(a, base, at)
        if at + SUB < base + BLK:
            take_off(a, slice(at, at + SUB), slice(at + SUB, base + BLK), slice(base, end))
    if base + BLK < R:
        take_off(a, slice(base, base + BLK), slice(base + BLK, R), slice(base + BLK, end))


def refresh_kernel(
    bc_ref, g_hbm, sb_hbm, o_ref,
    g_ref, sb_ref, om, ghi, glo, part, yrecv, q, zrecv, s, st, gp, gr, gz, gbuf, c, ck, d, dx, e, ez,
    a, yb, yr, hz, ob, send, recv, local,
):
    f, t, z, j, x, k, y, h = position()
    rows, cols = g_ref.shape
    m, zz = y * NJ + j, h * NZ + z

    def at_z(dd):
        w = lax.rem(zz + dd, NT)
        return lax.rem(w, NZ) * NJ + j, lax.div(w, NZ) * NY + y

    def zl(dd):
        return lax.rem(z + dd, NZ)

    def at_zl(dd):
        return zl(dd) * NJ + j, t

    def ml(dd):
        return lax.rem(m + dd, NM)

    def at_m(dd):
        w = ml(dd)
        return z * NJ + lax.rem(w, NJ), h * NY + lax.div(w, NJ)

    def jl(dd):
        return lax.rem(j + dd, NJ)

    def at_j(dd):
        return z * NJ + jl(dd), t

    def yl(dd):
        return lax.rem(y + dd, NY)

    def at_y(dd):
        return f, h * NY + yl(dd)

    def xl(dd):
        return lax.rem(x + dd, NX)

    def at_yx(dy, dx):
        return z * NJ + xl(dx) * NK + k, h * NY + yl(dy)

    partner = (z * NJ + x * NK + 1 - k, t)
    loads = [
        pltpu.make_async_copy(g_hbm, g_ref, local.at[0]),
        pltpu.make_async_copy(sb_hbm, sb_ref, local.at[1]),
    ]
    for load in loads:
        load.start()
    peers = [at_m(dd) for dd in range(1, NM)] + [at_z(dd) for dd in range(1, NT)]
    barrier = pltpu.get_barrier_semaphore()
    for peer in peers:
        pl.semaphore_signal(barrier, inc=1, device_id=peer, device_id_type=MESH)

    for load in loads:
        load.wait()
    for b in range(cols // BLK):
        sign = (2 * sb_ref[b * BLK:(b + 1) * BLK, :] - 1).astype(F32)
        for cb in range(R // BLK):
            here = jnp.where(bc_ref[b] == cb, 1.0, 0.0).astype(F32)
            om[b * BLK:(b + 1) * BLK, cb * BLK:(cb + 1) * BLK] = (sign * here).astype(BF16)
    hi, lo = split(g_ref[...])
    ghi[...] = hi
    glo[...] = lo
    for b in range(NB):
        pick = slice(b * BLK, (b + 1) * BLK)
        part[b] = (dot(ghi[...], om[:, pick]) + dot(glo[...], om[:, pick])).reshape(NY, rows // NY, BLK)
    pl.semaphore_wait(barrier, len(peers))
    net = Sender(send, recv)

    order = (2, 1, 3)
    over_y = [
        [net.put(part.at[b, yl(dd)], yrecv.at[b, dd - 1], at_y(dd)) for dd in order] for b in range(NB)
    ]
    over_z = []
    for b in range(NB):
        arrive(over_y[b])
        q[b] = part[b, y] + yrecv[b, 0] + yrecv[b, 1] + yrecv[b, 2]
        over_z.append(net.put(q.at[b], zrecv.at[b], at_z(NZ)))
    slab = []
    mine = []
    for b in range(NB):
        arrive([over_z[b]])
        mine.append(q[b] + zrecv[b])
        s[b, y] = mine[b]
        if b < 2:
            slab += [net.put(s.at[b, y], s.at[b, y], at_y(dd)) for dd in order]

    upper = [
        jnp.dot(
            mine[b].T,
            jnp.concatenate(mine[b:], axis=1),
            precision=HIGHEST,
            preferred_element_type=F32,
        )
        for b in range(NB)
    ]
    first_half = (jnp.zeros((8, BLK), jnp.int32) + h) == 0
    tiles = [
        [upper[rb][8 * r:8 * r + 8, (cb - rb) * BLK:(cb - rb + 1) * BLK] for rb, r, cb in owned(w)]
        for w in range(NM)
    ]
    gram_m = []
    for n in range(3):
        for w in range(NM):
            gp[n, w] = jnp.where(first_half, tiles[w][n], tiles[w][3 + n] if n < 2 else 0.0)
        gram_m.append([net.put(gp.at[n, ml(dd)], gr.at[n, dd - 1], at_m(dd)) for dd in range(1, NM)])
    for b in range(2, NB):
        slab += [net.put(s.at[b, y], s.at[b, y], at_y(dd)) for dd in order]
    gram_z = []
    for n in range(3):
        arrive(gram_m[n])
        total = gp[n, m]
        for dd in range(1, NM):
            total = total + gr[n, dd - 1]
        gz[n, h, z] = total
        gram_z.append([net.put(gz.at[n, h, z], gz.at[n, h, z], at_z(dd)) for dd in range(1, NT)])

    arrive(slab)
    for b in range(NB):
        st[b * BLK:(b + 1) * BLK, :] = s[b].reshape(rows, BLK).T
    shi, slo = split(st[...])
    for n in range(cols // 256):
        gh, gl = ghi[:, n * 256:(n + 1) * 256], glo[:, n * 256:(n + 1) * 256]
        c[:, :, :, n * 256:(n + 1) * 256] = (dot(shi, gh) + (dot(shi, gl) + dot(slo, gh))).reshape(
            NX, NK, R // NJ, 256
        )
    arrive([net.put(c.at[:, 1 - k], ck, partner)])
    d[...] = c[:, k] + ck[...]
    c_x = [net.put(d.at[xl(dd)], dx.at[dd - 1], at_yx(0, dd)) for dd in range(1, NX)]

    near = [(dy, dd) for dy in range(NY) for dd in range(NX) if dy or dd]
    gram_yx, gram_k = [], []
    for n in range(3):
        arrive(gram_z[n])
        for half in range(NH):
            total = gz[n, half, 0]
            for i in range(1, NZ):
                total = total + gz[n, half, i]
            gbuf[n, half, y, x, k] = total
        own = gbuf.at[n, :, y, x, k]
        gram_yx.append([net.put(own, own, at_yx(dy, dd)) for dy, dd in near])
        gram_k.append(net.put(own, own, partner))
    for n in range(3):
        for (dy, dd), copy in zip(near, gram_yx[n]):
            copy.wait_recv()
            came = gbuf.at[n, :, lax.rem(y + NY - dy, NY), lax.rem(x + NX - dd, NX), k]
            gram_k.append(net.put(came, came, partner))
    arrive(c_x)
    total = d[x] + dx[0] + dx[1] + dx[2]
    for n in range(NZ):
        e[n] = total[:, n * BLK:(n + 1) * BLK]
    c_z = [net.put(e.at[zl(dd)], ez.at[dd - 1], at_zl(dd)) for dd in range(1, NZ)]
    arrive(gram_k)

    for b in range(1, NB):
        a[b * BLK:(b + 1) * BLK, 0:b * BLK] = jnp.zeros((BLK, b * BLK), F32)
    for w in range(NM):
        from_m = w // NJ, w // NK % NX, w % NK
        for n, (rb, r, cb) in enumerate(owned(w)):
            at = rb * BLK + 8 * r
            a[at:at + 8, cb * BLK:(cb + 1) * BLK] = gbuf[(n % 3, n // 3, *from_m)]
    chunk = R // NJ
    down = lax.broadcasted_iota(jnp.int32, (R, BLK), 0) - chunk * j
    across = lax.broadcasted_iota(jnp.int32, (R, BLK), 1)
    a[:, R:] = jnp.where((down == across) & (across < chunk), 1.0, 0.0)
    last = R - BLK
    for base in range(0, last, BLK):
        factor(a, base)
    arrive(c_z)
    product = e[z]
    for dd in range(1, NZ):
        product = product + ez[dd - 1]

    def solved(first, after):
        return jnp.dot(
            a[first:after, R:R + chunk], product, precision=HIGHEST, preferred_element_type=F32
        ).reshape((after - first) // BLK * 2, NJ, 8, BLK)

    cut = last // (8 * NJ)
    early, late = pl.ds(0, cut), pl.ds(cut, NZ - cut)
    yb[0:cut] = solved(0, last)
    sums = [[net.put(yb.at[early, jl(dd)], yr.at[dd - 1, early], at_j(dd)) for dd in range(1, NJ)]]
    factor(a, last)
    yb[cut:NZ] = solved(last, R)
    sums.append([net.put(yb.at[late, jl(dd)], yr.at[dd - 1, late], at_j(dd)) for dd in range(1, NJ)])
    for part_sums, span in zip(sums, (early, late)):
        arrive(part_sums)
        total = yb[span, j]
        for dd in range(1, NJ):
            total = total + yr[dd - 1, span]
        hz[span] = total
    ob[z] = hz[z]
    arrive([net.put(hz.at[zl(dd)], ob.at[z], at_zl(dd)) for dd in range(1, NZ)])
    for n in range(NZ):
        o_ref[:, n * BLK:(n + 1) * BLK] = ob[n]
    net.drain()


def shards(gradient, sign_bits, block_column):
    rows, cols = gradient.shape
    vmem = pl.BlockSpec(memory_space=pltpu.VMEM)
    hbm = pl.BlockSpec(memory_space=pltpu.HBM)
    n_sems = 296
    gram_shape = (3, NH, NY, NX, NK, 8, BLK)
    return pl.pallas_call(
        refresh_kernel,
        out_shape=jax.ShapeDtypeStruct((R // (NZ * NJ), cols), F32),
        in_specs=[pl.BlockSpec(memory_space=pltpu.SMEM), hbm, hbm],
        out_specs=vmem,
        scratch_shapes=[
            pltpu.VMEM((rows, cols), F32),
            pltpu.VMEM((cols, BLK), jnp.int32),
            pltpu.VMEM((cols, R), BF16),
            pltpu.VMEM((rows, cols), BF16),
            pltpu.VMEM((rows, cols), BF16),
            pltpu.VMEM((NB, NY, rows // NY, BLK), F32),
            pltpu.VMEM((NB, NY - 1, rows // NY, BLK), F32),
            pltpu.VMEM((NB, rows // NY, BLK), F32),
            pltpu.VMEM((NB, rows // NY, BLK), F32),
            pltpu.VMEM((NB, NY, rows // NY, BLK), F32),
            pltpu.VMEM((R, rows), F32),
            pltpu.VMEM((3, NM, 8, BLK), F32),
            pltpu.VMEM((3, NM - 1, 8, BLK), F32),
            pltpu.VMEM((3, NH, NZ, 8, BLK), F32),
            pltpu.VMEM(gram_shape, F32),
            pltpu.VMEM((NX, NK, R // NJ, cols), F32),
            pltpu.VMEM((NX, R // NJ, cols), F32),
            pltpu.VMEM((NX, R // NJ, cols), F32),
            pltpu.VMEM((NX - 1, R // NJ, cols), F32),
            pltpu.VMEM((NZ, R // NJ, BLK), F32),
            pltpu.VMEM((NZ - 1, R // NJ, BLK), F32),
            pltpu.VMEM((R, R + BLK), F32),
            pltpu.VMEM((NZ, NJ, 8, BLK), F32),
            pltpu.VMEM((NJ - 1, NZ, 8, BLK), F32),
            pltpu.VMEM((NZ, 8, BLK), F32),
            pltpu.VMEM((NZ, 8, BLK), F32),
            pltpu.SemaphoreType.DMA((n_sems,)),
            pltpu.SemaphoreType.DMA((n_sems,)),
            pltpu.SemaphoreType.DMA((2,)),
        ],
        compiler_params=pltpu.CompilerParams(
            collective_id=0, has_side_effects=True
        ),
        name="refresh",
    )(block_column, gradient, sign_bits)


def solution(mesh):
    return jax.shard_map(
        shards,
        mesh=mesh,
        in_specs=(P("fsdp", "tp"), P("tp", None), P("tp")),
        out_specs=P("fsdp", "tp"),
        check_vma=False,
    )
```

```python
import functools

import jax
import jax.numpy as jnp
from jax import lax
from jax.experimental import pallas as pl
from jax.experimental.pallas import tpu as pltpu
from jax.sharding import PartitionSpec as P

MESH = pl.DeviceIdType.MESH
HIGHEST = lax.Precision.HIGHEST
F32 = jnp.float32
BF16 = jnp.bfloat16

R = 512
BLK = 128
SUB = 64
NZ, NX, NK, NY, NH = 8, 4, 2, 4, 2
NJ = NX * NK
NM = NY * NJ
NB = R // BLK
NT = NH * NZ


def position():
    f = lax.axis_index("fsdp")
    t = lax.axis_index("tp")
    j = lax.rem(f, NJ)
    return f, t, lax.div(f, NJ), j, lax.div(j, NK), lax.rem(j, NK), lax.rem(t, NY), lax.div(t, NY)


class Sender:
    def __init__(self, send, recv):
        self.send, self.recv, self.copies = send, recv, []

    def put(self, src, dst, device):
        i = len(self.copies)
        copy = pltpu.make_async_remote_copy(
            src_ref=src,
            dst_ref=dst,
            send_sem=self.send.at[i],
            recv_sem=self.recv.at[i],
            device_id=device,
            device_id_type=MESH,
        )
        copy.start()
        self.copies.append(copy)
        return copy

    def drain(self):
        for copy in self.copies:
            copy.wait_send()


def arrive(copies):
    for copy in copies:
        copy.wait_recv()


def split(v):
    hi = v.astype(BF16)
    return hi, (v - hi.astype(F32)).astype(BF16)


def dot(a, b):
    return jnp.dot(a, b, preferred_element_type=F32)


def strip(a, base, at):
    sub = lax.broadcasted_iota(jnp.int32, (8, BLK), 0)
    groups, tiles, lead = SUB // 8, (R + BLK - base) // BLK, at - base

    def spread(v):
        return jnp.broadcast_to(v, (8, BLK))

    def place(g, tile):
        return slice(at + 8 * g, at + 8 * g + 8), slice(base + BLK * tile, base + BLK * (tile + 1))

    rows = [[a[place(g, tile)] for tile in range(tiles)] for g in range(groups)]
    for g in range(groups):
        later = range(groups - g)
        lane = lead + 8 * g
        col = [[spread(rows[g + w][0][:, lane + i:lane + i + 1]) for i in range(8)] for w in later]
        for i in range(8):
            rs = lax.rsqrt(spread(col[0][i][i:i + 1, :]))
            l = [col[w][i] * rs for w in later]
            for n in range(i + 1, 8):
                ln = spread(col[0][i][n:n + 1, :]) * rs
                for w in later:
                    col[w][n] = col[w][n] - l[w] * ln
            low = jnp.where(sub > i, l[0], 0.0)
            for tile in range(tiles):
                row = spread(rows[g][tile][i:i + 1, :]) * rs
                rows[g][tile] = jnp.where(sub == i, row, rows[g][tile] - low * row)
                for w in later[1:]:
                    rows[g + w][tile] = rows[g + w][tile] - l[w] * row
    for g in range(groups):
        for tile in range(tiles):
            a[place(g, tile)] = rows[g][tile]


def owned(w):
    if w < 16:
        return [(0, w, 0), (0, w, 1), (0, w, 2), (0, w, 3), (3, 15 - w, 3)]
    return [(1, w - 16, 1), (1, w - 16, 2), (1, w - 16, 3), (2, 31 - w, 2), (2, 31 - w, 3)]


def take_off(a, done, rest, right):
    a[rest, right] = a[rest, right] - jnp.dot(
        a[done, rest].T, a[done, right], precision=HIGHEST, preferred_element_type=F32
    )


def factor(a, base):
    end = R + BLK
    for at in range(base, base + BLK, SUB):
        strip(a, base, at)
        if at + SUB < base + BLK:
            take_off(a, slice(at, at + SUB), slice(at + SUB, base + BLK), slice(base, end))
    if base + BLK < R:
        take_off(a, slice(base, base + BLK), slice(base + BLK, R), slice(base + BLK, end))


def refresh_kernel(
    bc_ref, g_hbm, sb_hbm, o_ref,
    g_ref, sb_ref, om, ghi, glo, part, yrecv, q, zrecv, s, st, gp, gr, gz, gbuf, c, ck, d, dx, e, ez,
    a, yb, yr, hz, ob, send, recv, local,
):
    f, t, z, j, x, k, y, h = position()
    rows, cols = g_ref.shape
    m, zz = y * NJ + j, h * NZ + z

    def at_z(dd):
        w = lax.rem(zz + dd, NT)
        return lax.rem(w, NZ) * NJ + j, lax.div(w, NZ) * NY + y

    def zl(dd):
        return lax.rem(z + dd, NZ)

    def at_zl(dd):
        return zl(dd) * NJ + j, t

    def ml(dd):
        return lax.rem(m + dd, NM)

    def at_m(dd):
        w = ml(dd)
        return z * NJ + lax.rem(w, NJ), h * NY + lax.div(w, NJ)

    def jl(dd):
        return lax.rem(j + dd, NJ)

    def at_j(dd):
        return z * NJ + jl(dd), t

    def yl(dd):
        return lax.rem(y + dd, NY)

    def at_y(dd):
        return f, h * NY + yl(dd)

    def xl(dd):
        return lax.rem(x + dd, NX)

    def at_yx(dy, dx):
        return z * NJ + xl(dx) * NK + k, h * NY + yl(dy)

    partner = (z * NJ + x * NK + 1 - k, t)
    loads = [
        pltpu.make_async_copy(g_hbm, g_ref, local.at[0]),
        pltpu.make_async_copy(sb_hbm, sb_ref, local.at[1]),
    ]
    for load in loads:
        load.start()
    peers = [at_m(dd) for dd in range(1, NM)] + [at_z(dd) for dd in range(1, NT)]
    barrier = pltpu.get_barrier_semaphore()
    for peer in peers:
        pl.semaphore_signal(barrier, inc=1, device_id=peer, device_id_type=MESH)

    for load in loads:
        load.wait()
    for b in range(cols // BLK):
        sign = (2 * sb_ref[b * BLK:(b + 1) * BLK, :] - 1).astype(F32)
        for cb in range(R // BLK):
            here = jnp.where(bc_ref[b] == cb, 1.0, 0.0).astype(F32)
            om[b * BLK:(b + 1) * BLK, cb * BLK:(cb + 1) * BLK] = (sign * here).astype(BF16)
    hi, lo = split(g_ref[...])
    ghi[...] = hi
    glo[...] = lo
    for b in range(NB):
        pick = slice(b * BLK, (b + 1) * BLK)
        part[b] = (dot(ghi[...], om[:, pick]) + dot(glo[...], om[:, pick])).reshape(NY, rows // NY, BLK)
    pl.semaphore_wait(barrier, len(peers))
    net = Sender(send, recv)

    order = (2, 1, 3)
    over_y = [
        [net.put(part.at[b, yl(dd)], yrecv.at[b, dd - 1], at_y(dd)) for dd in order] for b in range(NB)
    ]
    over_z = []
    for b in range(NB):
        arrive(over_y[b])
        q[b] = part[b, y] + yrecv[b, 0] + yrecv[b, 1] + yrecv[b, 2]
        over_z.append(net.put(q.at[b], zrecv.at[b], at_z(NZ)))
    slab = []
    mine = []
    for b in range(NB):
        arrive([over_z[b]])
        mine.append(q[b] + zrecv[b])
        s[b, y] = mine[b]
        if b < 2:
            slab += [net.put(s.at[b, y], s.at[b, y], at_y(dd)) for dd in order]

    upper = [
        jnp.dot(
            mine[b].T,
            jnp.concatenate(mine[b:], axis=1),
            precision=HIGHEST,
            preferred_element_type=F32,
        )
        for b in range(NB)
    ]
    first_half = (jnp.zeros((8, BLK), jnp.int32) + h) == 0
    for w in range(NM):
        tiles = [upper[rb][8 * r:8 * r + 8, (cb - rb) * BLK:(cb - rb + 1) * BLK] for rb, r, cb in owned(w)]
        gp[w, 0] = jnp.where(first_half, tiles[0], tiles[3])
        gp[w, 1] = jnp.where(first_half, tiles[1], tiles[4])
        gp[w, 2] = jnp.where(first_half, tiles[2], 0.0)
    gram_m = [net.put(gp.at[ml(dd)], gr.at[dd - 1], at_m(dd)) for dd in range(1, NM)]
    for b in range(2, NB):
        slab += [net.put(s.at[b, y], s.at[b, y], at_y(dd)) for dd in order]
    arrive(gram_m)
    total = gp[m]
    for dd in range(1, NM):
        total = total + gr[dd - 1]
    gz[h, z] = total
    gram_z = [net.put(gz.at[h, z], gz.at[h, z], at_z(dd)) for dd in range(1, NT)]

    arrive(slab)
    for b in range(NB):
        st[b * BLK:(b + 1) * BLK, :] = s[b].reshape(rows, BLK).T
    shi, slo = split(st[...])
    for n in range(cols // 256):
        gh, gl = ghi[:, n * 256:(n + 1) * 256], glo[:, n * 256:(n + 1) * 256]
        c[:, :, :, n * 256:(n + 1) * 256] = (dot(shi, gh) + (dot(shi, gl) + dot(slo, gh))).reshape(
            NX, NK, R // NJ, 256
        )
    arrive([net.put(c.at[:, 1 - k], ck, partner)])
    d[...] = c[:, k] + ck[...]
    c_x = [net.put(d.at[xl(dd)], dx.at[dd - 1], at_yx(0, dd)) for dd in range(1, NX)]

    arrive(gram_z)
    for half in range(NH):
        total = gz[half, 0]
        for i in range(1, NZ):
            total = total + gz[half, i]
        gbuf[half, y, x, k] = total
    near = [(dy, dd) for dy in range(NY) for dd in range(NX) if dy or dd]
    gram_yx = [net.put(gbuf.at[:, y, x, k], gbuf.at[:, y, x, k], at_yx(dy, dd)) for dy, dd in near]
    gram_k = [net.put(gbuf.at[:, y, x, k], gbuf.at[:, y, x, k], partner)]
    arrive(c_x)
    total = d[x] + dx[0] + dx[1] + dx[2]
    for n in range(NZ):
        e[n] = total[:, n * BLK:(n + 1) * BLK]
    c_z = [net.put(e.at[zl(dd)], ez.at[dd - 1], at_zl(dd)) for dd in range(1, NZ)]
    for (dy, dd), copy in zip(near, gram_yx):
        copy.wait_recv()
        ys, xs = lax.rem(y + NY - dy, NY), lax.rem(x + NX - dd, NX)
        gram_k.append(net.put(gbuf.at[:, ys, xs, k], gbuf.at[:, ys, xs, k], partner))
    arrive(gram_k)

    for b in range(1, NB):
        a[b * BLK:(b + 1) * BLK, 0:b * BLK] = jnp.zeros((BLK, b * BLK), F32)
    for w in range(NM):
        from_m = w // NJ, w // NK % NX, w % NK
        for n, (rb, r, cb) in enumerate(owned(w)):
            at = rb * BLK + 8 * r
            a[at:at + 8, cb * BLK:(cb + 1) * BLK] = gbuf[(n // 3, *from_m, n % 3)]
    chunk = R // NJ
    down = lax.broadcasted_iota(jnp.int32, (R, BLK), 0) - chunk * j
    across = lax.broadcasted_iota(jnp.int32, (R, BLK), 1)
    a[:, R:] = jnp.where((down == across) & (across < chunk), 1.0, 0.0)
    last = R - BLK
    for base in range(0, last, BLK):
        factor(a, base)
    arrive(c_z)
    product = e[z]
    for dd in range(1, NZ):
        product = product + ez[dd - 1]

    def solved(first, after):
        return jnp.dot(
            a[first:after, R:R + chunk], product, precision=HIGHEST, preferred_element_type=F32
        ).reshape((after - first) // BLK * 2, NJ, 8, BLK)

    cut = last // (8 * NJ)
    early, late = pl.ds(0, cut), pl.ds(cut, NZ - cut)
    yb[0:cut] = solved(0, last)
    sums = [[net.put(yb.at[early, jl(dd)], yr.at[dd - 1, early], at_j(dd)) for dd in range(1, NJ)]]
    factor(a, last)
    yb[cut:NZ] = solved(last, R)
    sums.append([net.put(yb.at[late, jl(dd)], yr.at[dd - 1, late], at_j(dd)) for dd in range(1, NJ)])
    for part_sums, span in zip(sums, (early, late)):
        arrive(part_sums)
        total = yb[span, j]
        for dd in range(1, NJ):
            total = total + yr[dd - 1, span]
        hz[span] = total
    ob[z] = hz[z]
    arrive([net.put(hz.at[zl(dd)], ob.at[z], at_zl(dd)) for dd in range(1, NZ)])
    for n in range(NZ):
        o_ref[:, n * BLK:(n + 1) * BLK] = ob[n]
    net.drain()


def shards(gradient, sign_bits, block_column):
    rows, cols = gradient.shape
    vmem = pl.BlockSpec(memory_space=pltpu.VMEM)
    hbm = pl.BlockSpec(memory_space=pltpu.HBM)
    n_sems = 144
    gram_shape = (NH, NY, NX, NK, 3, 8, BLK)
    return pl.pallas_call(
        refresh_kernel,
        out_shape=jax.ShapeDtypeStruct((R // (NZ * NJ), cols), F32),
        in_specs=[pl.BlockSpec(memory_space=pltpu.SMEM), hbm, hbm],
        out_specs=vmem,
        scratch_shapes=[
            pltpu.VMEM((rows, cols), F32),
            pltpu.VMEM((cols, BLK), jnp.int32),
            pltpu.VMEM((cols, R), BF16),
            pltpu.VMEM((rows, cols), BF16),
            pltpu.VMEM((rows, cols), BF16),
            pltpu.VMEM((NB, NY, rows // NY, BLK), F32),
            pltpu.VMEM((NB, NY - 1, rows // NY, BLK), F32),
            pltpu.VMEM((NB, rows // NY, BLK), F32),
            pltpu.VMEM((NB, rows // NY, BLK), F32),
            pltpu.VMEM((NB, NY, rows // NY, BLK), F32),
            pltpu.VMEM((R, rows), F32),
            pltpu.VMEM((NM, 3, 8, BLK), F32),
            pltpu.VMEM((NM - 1, 3, 8, BLK), F32),
            pltpu.VMEM((NH, NZ, 3, 8, BLK), F32),
            pltpu.VMEM(gram_shape, F32),
            pltpu.VMEM((NX, NK, R // NJ, cols), F32),
            pltpu.VMEM((NX, R // NJ, cols), F32),
            pltpu.VMEM((NX, R // NJ, cols), F32),
            pltpu.VMEM((NX - 1, R // NJ, cols), F32),
            pltpu.VMEM((NZ, R // NJ, BLK), F32),
            pltpu.VMEM((NZ - 1, R // NJ, BLK), F32),
            pltpu.VMEM((R, R + BLK), F32),
            pltpu.VMEM((NZ, NJ, 8, BLK), F32),
            pltpu.VMEM((NJ - 1, NZ, 8, BLK), F32),
            pltpu.VMEM((NZ, 8, BLK), F32),
            pltpu.VMEM((NZ, 8, BLK), F32),
            pltpu.SemaphoreType.DMA((n_sems,)),
            pltpu.SemaphoreType.DMA((n_sems,)),
            pltpu.SemaphoreType.DMA((2,)),
        ],
        compiler_params=pltpu.CompilerParams(
            collective_id=0, has_side_effects=True
        ),
        name="refresh",
    )(block_column, gradient, sign_bits)


def solution(mesh):
    return jax.shard_map(
        shards,
        mesh=mesh,
        in_specs=(P("fsdp", "tp"), P("tp", None), P("tp")),
        out_specs=P("fsdp", "tp"),
        check_vma=False,
    )
```
